32 devices in a mesh: mem: 8 (over y, x, core), space: 4 (over z).
Axes of the slice: x: 2, y: 2, z: 4, core: 2. Of those that a mesh axis runs over, the one named last changes fastest.
Arguments:
- ensemble: float32 [96, 3, 16, 1024], P('mem', None, 'space'), may hold values from -1.8 to 1.8
- sea_depth: float32 [16, 1024], P('space'), may hold values from 0.5 to 2
- ocean_mask: int32 [16, 1024], P('space'), may hold values 0 or 1
- observed_cells: int32 [4, 128], P('space'), may hold values from 0 to 4095
- observed_values: float32 [4, 128], P('space'), may hold values from -6 to 6
- observed_error: float32 [4, 128], P('space'), may hold values from 0.5 to 2
Outputs:
- analysis: float32 [96, 3, 16, 1024], P('mem', None, 'space')
The draws below stay inside these ranges and needn't reach their ends.
Inputs may be any that keep to these rules, and one draw needn't show every extreme that they name: `observed_cells`: indices are local to the slab; an observation may repeat a cell.
All inputs are finite; a program needn't handle non-finite values. No bound on the sum of `ocean_mask` on one device may be relied on, other than what follows from the above.
Results may differ from the reference program's by a relative error of at most 0.00021.
Values sent between devices are 32-bit elements; how exact they have to be, the bound alone decides.
A program may use at most 64 MiB of HBM per device.

```python
import math
import jax
import jax.numpy as jnp
from jax import lax

ENS = 96
CX = 4
NY = 1024
OBS = 128
STEPS = 3
NS_ITERS = 6
NX = 16
N_SPACE = 4


def with_ends(drawn, own_key, least, high):
    dims = drawn.shape
    index_at = [jax.random.randint(jax.random.fold_in(own_key, axis), (), 0, dims[axis]) for axis in range(len(dims))]
    drawn = drawn.at[tuple(index_at)].set(least)
    longest = dims.index(max(dims))
    index_at[longest] = (index_at[longest] + 1) % dims[longest]
    return drawn.at[tuple(index_at)].set(high)


def block_scale(rng, extent, split, low, top_value):
    loudness, own = 1.0, jax.random.fold_in(rng, 6)
    for dim, shards_of in split:
        steps = jnp.exp(jax.random.uniform(jax.random.fold_in(own, dim), (shards_of,), jnp.float32, low / len(split), top_value / len(split)))
        loudness = loudness * jnp.repeat(steps, extent[dim] // shards_of).reshape([-1 if axis == dim else 1 for axis in range(len(extent))])
    return loudness


def centred(own_key, shape, width, reach, cuts=(), kind=jnp.bfloat16):
    array = jax.random.normal(own_key, shape, jnp.float32) * width
    if len(cuts) > 0:
        array = block_scale(own_key, shape, cuts, -0.22, 0.18) * array
    return jnp.clip(array, min=-reach, max=reach).astype(kind)


def setup_inputs(seed: int = 0) -> dict:
    key_list = jax.random.split(jax.random.key(seed), 7)
    return {
        "ensemble": centred(key_list[0], (ENS, 3, NX, NY), 0.3, 1.8, ((0, 8), (2, 4)), jnp.float32),
        "sea_depth": jnp.clip(jnp.exp(math.log(2.0) - 1.3862944 * jax.random.uniform(key_list[1], (NX, NY), jnp.float32) ** block_scale(key_list[1], (NX, NY), ((0, 4),), -0.2, 0.2)), 0.5, 2.0),
        "ocean_mask": with_ends((jax.random.randint(key_list[2], (NX, NY), 0, 10) < 9).astype(jnp.int32), jax.random.fold_in(key_list[2], 1), 0, 1),
        "observed_cells": with_ends(jax.random.randint(key_list[3], (N_SPACE, OBS), 0, CX * NY), jax.random.fold_in(key_list[3], 1), 0, (CX * NY) - 1).astype(jnp.int32),
        "observed_values": centred(key_list[4], (N_SPACE, OBS), 1.0, 6.0, ((0, 4),), jnp.float32),
        "observed_error": jnp.clip(jnp.exp(math.log(2.0) - 1.3862944 * jax.random.uniform(key_list[5], (N_SPACE, OBS), jnp.float32) ** block_scale(key_list[5], (N_SPACE, OBS), ((0, 4),), -0.2, 0.2)), 0.5, 2.0),
    }


GRAV = 1.0
DT = 0.3
VISC = 0.1

def east(field):
    return (jnp.roll(field, -1, axis=-2) - jnp.roll(field, 1, axis=-2)) * 0.5

def north(field):
    return (jnp.roll(field, -1, axis=-1) - jnp.roll(field, 1, axis=-1)) * 0.5

def spread(field):
    return jnp.roll(field, -1, axis=-2) + jnp.roll(field, 1, axis=-2) + jnp.roll(field, 1, axis=-1) + jnp.roll(field, -1, axis=-1) - 4.0 * field

def advance(state, sea_depth, ocean, coriolis):
    height = state[:, 0]
    along = state[:, 1]
    across = state[:, 2]
    total = sea_depth + height
    fresh = height - DT * (east(total * along) + north(total * across))
    tend_along = GRAV * east(fresh) + along * east(along) + across * north(along) - coriolis * across
    tend_across = GRAV * north(fresh) + along * east(across) + across * north(across) + coriolis * along
    along_new = (along - DT * tend_along + DT * VISC * spread(along)) * ocean
    across_new = (across - DT * tend_across + DT * VISC * spread(across)) * ocean
    return jnp.stack([fresh, along_new, across_new], axis=1)

def inverse_root(matrix, sweeps):
    norm_scale = jnp.sqrt(jnp.sum(matrix * matrix))
    identity = jnp.eye(matrix.shape[0], dtype=jnp.float32)
    iterate = matrix / norm_scale
    inverse = identity
    for sweep_index in range(sweeps):
        factor = 1.5 * identity - 0.5 * jnp.dot(inverse, iterate, precision=lax.Precision.HIGHEST)
        iterate = jnp.dot(iterate, factor, precision=lax.Precision.HIGHEST)
        inverse = jnp.dot(factor, inverse, precision=lax.Precision.HIGHEST)
    return inverse / jnp.sqrt(norm_scale)

def reference(ensemble, sea_depth, ocean_mask, observed_cells, observed_values, observed_error):
    ocean = ocean_mask.astype(jnp.float32)
    coriolis = 0.05 + 0.1 * jnp.arange(NY, dtype=jnp.float32) / NY
    state = ensemble
    for step_index in range(STEPS):
        state = advance(state, sea_depth, ocean, coriolis)
    members = state.shape[0]
    heights = state[:, 0].reshape(members, N_SPACE, CX * NY)
    picked = jax.vmap(lambda rows, where: jnp.take(rows, where, axis=1), in_axes=(1, 0), out_axes=1)(heights, observed_cells.astype(jnp.int32))
    picked = picked.reshape(members, N_SPACE * OBS)
    errors = observed_error.reshape(N_SPACE * OBS)
    values = observed_values.reshape(N_SPACE * OBS)
    hmean = lax.optimization_barrier(jnp.mean(picked, axis=0))
    scaled = (picked - hmean) / errors
    misfit = (values - hmean) / errors
    gram = jnp.dot(scaled, scaled.T, precision=lax.Precision.HIGHEST)
    drive = jnp.dot(scaled, misfit, precision=lax.Precision.HIGHEST)
    identity = jnp.eye(members, dtype=jnp.float32)
    weights = inverse_root(identity + gram / (members - 1), NS_ITERS)
    mean_weight = jnp.dot(weights, jnp.dot(weights, drive, precision=lax.Precision.HIGHEST), precision=lax.Precision.HIGHEST) / (members - 1)
    combined = weights + mean_weight[:, None]
    flat = state.reshape(members, -1)
    center = lax.optimization_barrier(jnp.mean(flat, axis=0))
    result = center + jnp.dot(combined.T, flat - center, precision=lax.Precision.HIGHEST)
    return result.reshape(state.shape)
```

```python
import functools

import jax
import jax.numpy as jnp
from jax import lax
from jax.experimental import pallas as pl
from jax.experimental.pallas import tpu as pltpu
from jax.sharding import PartitionSpec as P

STEPS = 3
NS_ITERS = 6
GRAV = 1.0
DT = 0.3
VISC = 0.1
SUB = 8
HIGHEST = lax.Precision.HIGHEST
MESH = pl.DeviceIdType.MESH


def pieces(x):
    found = []
    for _ in range(3):
        part = x.astype(jnp.bfloat16)
        found.append(part)
        x = x - part.astype(jnp.float32)
    return found


def dot(a, b, contract=((1,), (0,))):
    def mul(x, y):
        return lax.dot_general(x, y, (contract, ((), ())), preferred_element_type=jnp.float32)

    a0, a1, a2 = pieces(a)
    b0, b1, b2 = pieces(b)
    small = (mul(a0, b2) + mul(a2, b0)) + mul(a1, b1)
    return (small + (mul(a0, b1) + mul(a1, b0))) + mul(a0, b0)


def kernel(
    dims,
    ens,
    depth,
    ocean_ref,
    cells,
    obs,
    out,
    state,
    fresh,
    hsend,
    hrecv,
    hot,
    split,
    picks,
    zpicks,
    mpicks,
    zobs,
    frecv,
    full,
    rback,
    h_ss,
    h_rs,
    o_ss,
    o_rs,
    z_ss,
    z_rs,
    m_ss,
    m_rs,
    f_ss,
    f_rs,
    b_ss,
    b_rs,
):
    n_mem, n_space, groups, gs, rows, cols, n_obs = dims
    members = n_mem * groups * gs
    padded = n_mem * groups * SUB
    per = rows * cols // n_mem
    i_mem = lax.axis_index("mem")
    i_space = lax.axis_index("space")

    barrier = pltpu.get_barrier_semaphore()
    for k in range(1, n_space):
        pl.semaphore_signal(
            barrier, inc=1, device_id={"space": lax.rem(i_space + k, n_space)}, device_id_type=MESH
        )
    for k in range(1, n_mem):
        pl.semaphore_signal(
            barrier, inc=1, device_id={"mem": lax.rem(i_mem + k, n_mem)}, device_id_type=MESH
        )
    pl.semaphore_wait(barrier, n_space - 1 + n_mem - 1)

    def remote(src, dst, ss, rs, where):
        return pltpu.make_async_remote_copy(
            src_ref=src, dst_ref=dst, send_sem=ss, recv_sem=rs, device_id=where, device_id_type=MESH
        )

    def to_space(k):
        return {"space": lax.rem(i_space + k, n_space)}

    def to_mem(k):
        return {"mem": lax.rem(i_mem + k, n_mem)}

    def nxt(x):
        return pltpu.roll(x, cols - 1, 1)

    def prv(x):
        return pltpu.roll(x, 1, 1)

    def north(x):
        return (nxt(x) - prv(x)) * 0.5

    coriolis = 0.05 + 0.1 * lax.broadcasted_iota(jnp.int32, (1, cols), 1).astype(jnp.float32) / cols
    half = DT * 0.5

    def get(step, g, field, r):
        if step == 0:
            return ens[g, field, r]
        return state[(step - 1) % 2, g, field, r]

    def total(step, g, r):
        return depth[pl.ds(r, 1), :] + get(step, g, 0, r)

    def halo_copies(step, g):
        found = []
        for d, k in ((0, n_space - 1), (1, 1)):
            found.append(
                remote(
                    hsend.at[step, g, d],
                    hrecv.at[step, g, d],
                    h_ss.at[step, g, d],
                    h_rs.at[step, g, d],
                    to_space(k),
                )
            )
        return found

    def send_edges(step, g):
        copies = halo_copies(step, g)
        for d, r, inner, sign in ((0, 0, 1, 1.0), (1, rows - 1, rows - 2, -1.0)):
            u, v = get(step, g, 1, r), get(step, g, 2, r)
            tot = total(step, g, r)
            inner_flux = total(step, g, inner) * get(step, g, 1, inner)
            hsend[step, g, d, 0] = u
            hsend[step, g, d, 1] = v
            hsend[step, g, d, 2] = tot * u
            hsend[step, g, d, 3] = get(step, g, 0, r) - (sign * half) * inner_flux - DT * north(tot * v)
            copies[d].start()

    def advance(step, g):
        for r in range(1, rows - 1):
            flux = [total(step, g, q) * get(step, g, 1, q) for q in (r - 1, r + 1)]
            fresh[r + 1] = (
                get(step, g, 0, r)
                - half * (flux[1] - flux[0])
                - DT * north(total(step, g, r) * get(step, g, 2, r))
            )
        copies = halo_copies(step, g)
        for d in (0, 1):
            copies[d].wait_recv()
        above, below = hrecv.at[step, g, 0], hrecv.at[step, g, 1]
        fresh[0] = below[3] - half * hsend[step, g, 0, 2]
        fresh[1] = hsend[step, g, 0, 3] + half * below[2]
        fresh[rows] = hsend[step, g, 1, 3] - half * above[2]
        fresh[rows + 1] = above[3] + half * hsend[step, g, 1, 2]

        def row(field, r):
            if r < 0:
                return below[field - 1]
            if r == rows:
                return above[field - 1]
            return get(step, g, field, r)

        slot = step % 2
        for r in range(rows):
            ocean = ocean_ref[pl.ds(r, 1), :]
            u, v = row(1, r), row(2, r)
            here = fresh[r + 1]
            state[slot, g, 0, r] = here
            for field, f, push, turn in (
                (1, u, (fresh[r + 2] - fresh[r]) * 0.5, -(coriolis * v)),
                (2, v, north(here), coriolis * u),
            ):
                up, down = row(field, r + 1), row(field, r - 1)
                right, left = nxt(f), prv(f)
                tend = GRAV * push + u * ((up - down) * 0.5) + v * ((right - left) * 0.5) + turn
                lap = up + down + right + left - 4.0 * f
                state[slot, g, field, r] = (f - DT * tend + DT * VISC * lap) * ocean

    last = (STEPS - 1) % 2

    def forward_copies(g):
        found = []
        for k in range(1, n_mem):
            first = lax.rem(i_mem + k, n_mem) * per
            found.append(
                remote(
                    state.at[last, g, :, first // cols, :, pl.ds(pl.multiple_of(lax.rem(first, cols), 128), per)],
                    frecv.at[g, k],
                    f_ss.at[g, k],
                    f_rs.at[g, k],
                    to_mem(k),
                )
            )
        return found

    obs_copies = [
        remote(obs, zobs.at[k], o_ss.at[k], o_rs.at[k], to_space(k)) for k in range(1, n_space)
    ]
    for g in range(groups):
        send_edges(0, g)
    for copy in obs_copies:
        copy.start()

    wanted = cells[...]
    for c in range(rows * cols // 128):
        index = lax.broadcasted_iota(jnp.int32, (128, n_obs), 0) + c * 128
        hot[pl.ds(c * 128, 128), :] = jnp.where(index == wanted, 1.0, 0.0).astype(jnp.bfloat16)
    split[...] = jnp.zeros_like(split)
    full[...] = jnp.zeros_like(full)

    for step in range(STEPS):
        for g in range(groups):
            advance(step, g)
            if step < STEPS - 1:
                send_edges(step + 1, g)
            else:
                for r in range(rows):
                    h = state[last, g, 0, r]
                    for p in range(3):
                        part = h.astype(jnp.bfloat16).astype(jnp.float32)
                        split[pl.ds((p * groups + g) * SUB, gs), pl.ds(r * cols, cols)] = part
                        h = h - part
                if g < groups - 1:
                    for copy in forward_copies(g):
                        copy.start()

    three = jnp.dot(split[...].astype(jnp.bfloat16), hot[...], preferred_element_type=jnp.float32)
    size = groups * SUB
    mine = three[:size] + three[size : 2 * size] + three[2 * size :]
    for g in range(groups):
        picks[g] = mine[g * SUB : g * SUB + gs]
        zpicks[0, g] = mine[g * SUB : g * SUB + gs]
    z_copies = [
        remote(picks, zpicks.at[k], z_ss.at[k], z_rs.at[k], to_space(k)) for k in range(1, n_space)
    ]
    for copy in z_copies:
        copy.start()
    for copy in z_copies:
        copy.wait_recv()
    m_copies = [
        remote(zpicks, mpicks.at[k], m_ss.at[k], m_rs.at[k], to_mem(k)) for k in range(1, n_mem)
    ]
    for copy in m_copies:
        copy.start()
    for copy in forward_copies(groups - 1):
        copy.start()
    for copy in obs_copies:
        copy.wait_recv()
    for copy in m_copies:
        copy.wait_recv()

    row_id = lax.broadcasted_iota(jnp.int32, (padded, n_obs), 0)
    valid = lax.rem(row_id, SUB) < gs
    gap = jnp.zeros((SUB - gs, n_obs), jnp.float32)
    gram = jnp.zeros((padded, padded), jnp.float32)
    drive = jnp.zeros((padded, 1), jnp.float32)
    for s in range(n_space):
        for k in range(n_mem):
            for g in range(groups):
                piece = zpicks[s, g] if k == 0 else mpicks[k, s, g]
                full[0, pl.ds((k * groups + g) * SUB, gs), pl.ds(0, n_obs)] = piece
        raw = full[0, :, pl.ds(0, n_obs)]
        hmean = jnp.sum(raw, axis=0, keepdims=True) / members
        values = obs[pl.ds(0, 1), :] if s == 0 else zobs[s, pl.ds(0, 1), :]
        errors = obs[pl.ds(1, 1), :] if s == 0 else zobs[s, pl.ds(1, 1), :]
        scaled = jnp.where(valid, (raw - hmean) / errors, 0.0)
        misfit = (values - hmean) / errors
        gram = gram + dot(scaled, scaled, ((1,), (1,)))
        drive = drive + jnp.sum(scaled * misfit, axis=1, keepdims=True)

    r_id = lax.broadcasted_iota(jnp.int32, (padded, padded), 0)
    c_id = lax.broadcasted_iota(jnp.int32, (padded, padded), 1)
    identity = jnp.where(r_id == c_id, 1.0, 0.0)
    system = identity + gram / (members - 1)
    squares = jnp.where(lax.rem(r_id, SUB) < gs, system * system, 0.0)
    norm_sq = jnp.sum(jnp.sum(squares, axis=1, keepdims=True), axis=0, keepdims=True)
    norm_scale = jnp.sqrt(norm_sq)
    iterate = system / norm_scale
    factor = 1.5 * identity - 0.5 * iterate
    carry = (dot(iterate, factor), factor)

    def sweep(_, carry):
        iterate, inverse = carry
        factor = 1.5 * identity - 0.5 * dot(inverse, iterate)
        return dot(iterate, factor), dot(factor, inverse)

    iterate, inverse = lax.fori_loop(0, NS_ITERS - 2, sweep, carry)
    factor = 1.5 * identity - 0.5 * dot(inverse, iterate)
    weights = dot(factor, inverse) / jnp.sqrt(norm_scale)
    once = jnp.sum(weights * drive, axis=0, keepdims=True)
    mean_weight = jnp.sum(weights * once, axis=1, keepdims=True) / (members - 1)
    mixing = (weights + mean_weight).T

    my_first = i_mem * per
    my_row = my_first // cols
    my_cols = pl.ds(pl.multiple_of(lax.rem(my_first, cols), 128), per)
    fwd = [forward_copies(g) for g in range(groups)]
    for g in range(groups):
        for f in range(3):
            full[f, pl.ds(g * SUB, gs), :] = state[last, g, f, my_row, :, my_cols]
        for k in range(1, n_mem):
            fwd[g][k - 1].wait_recv()
            for f in range(3):
                full[f, pl.ds((k * groups + g) * SUB, gs), :] = frecv[g, k, f]

    back = {}
    for g in range(groups):
        for k in range(1, n_mem):
            back[g, k] = remote(
                rback.at[g, k],
                out.at[g, :, my_row, :, my_cols],
                b_ss.at[g, k],
                b_rs.at[g, k],
                to_mem(n_mem - k),
            )
    for f in range(3):
        whole = full[f]
        center = jnp.sum(whole, axis=0, keepdims=True) / members
        done = center + dot(mixing, whole - center)
        for k in range(n_mem):
            for g in range(groups):
                piece = done[(k * groups + g) * SUB : (k * groups + g) * SUB + gs]
                if k == 0:
                    out[g, f, my_row, :, my_cols] = piece
                else:
                    rback[g, k, f] = piece
    for copy in back.values():
        copy.start()

    for step in range(STEPS):
        for g in range(groups):
            for copy in halo_copies(step, g):
                copy.wait_send()
    for copy in obs_copies + z_copies + m_copies + sum(fwd, []):
        copy.wait_send()
    for copy in back.values():
        copy.wait()


def local(ensemble, sea_depth, ocean_mask, observed_cells, observed_values, observed_error):
    n_mem = lax.axis_size("mem")
    n_space = lax.axis_size("space")
    local_members, fields, rows, cols = ensemble.shape
    n_obs = observed_cells.shape[1]
    groups = 2
    gs = local_members // groups
    per = rows * cols // n_mem
    padded = n_mem * groups * SUB
    dims = (n_mem, n_space, groups, gs, rows, cols, n_obs)
    ens = ensemble.reshape(groups, gs, fields, rows, cols).transpose(0, 2, 3, 1, 4)
    ocean = ocean_mask.astype(jnp.float32)
    obs = jnp.concatenate([observed_values, observed_error], axis=0)
    f32 = jnp.float32
    dma = pltpu.SemaphoreType.DMA
    result = pl.pallas_call(
        functools.partial(kernel, dims),
        out_shape=jax.ShapeDtypeStruct(ens.shape, f32),
        in_specs=[pl.BlockSpec(memory_space=pltpu.VMEM)] * 5,
        out_specs=pl.BlockSpec(memory_space=pltpu.VMEM),
        scratch_shapes=[
            pltpu.VMEM((2, groups, 3, rows, gs, cols), f32),
            pltpu.VMEM((rows + 2, gs, cols), f32),
            pltpu.VMEM((STEPS, groups, 2, 4, gs, cols), f32),
            pltpu.VMEM((STEPS, groups, 2, 4, gs, cols), f32),
            pltpu.VMEM((rows * cols, n_obs), jnp.bfloat16),
            pltpu.VMEM((3 * groups * SUB, rows * cols), f32),
            pltpu.VMEM((groups, gs, n_obs), f32),
            pltpu.VMEM((n_space, groups, gs, n_obs), f32),
            pltpu.VMEM((n_mem, n_space, groups, gs, n_obs), f32),
            pltpu.VMEM((n_space, 2, n_obs), f32),
            pltpu.VMEM((groups, n_mem, 3, gs, per), f32),
            pltpu.VMEM((3, padded, per), f32),
            pltpu.VMEM((groups, n_mem, 3, gs, per), f32),
            dma((STEPS, groups, 2)),
            dma((STEPS, groups, 2)),
            dma((n_space,)),
            dma((n_space,)),
            dma((n_space,)),
            dma((n_space,)),
            dma((n_mem,)),
            dma((n_mem,)),
            dma((groups, n_mem)),
            dma((groups, n_mem)),
            dma((groups, n_mem)),
            dma((groups, n_mem)),
        ],
        compiler_params=pltpu.CompilerParams(
            collective_id=0, has_side_effects=True, vmem_limit_bytes=48 * 1024 * 1024
        ),
    )(ens, sea_depth, ocean, observed_cells, obs)
    return result.transpose(0, 3, 1, 2, 4).reshape(ensemble.shape)


def solution(mesh):
    return jax.shard_map(
        local,
        mesh=mesh,
        in_specs=(
            P("mem", None, "space", None),
            P("space", None),
            P("space", None),
            P("space", None),
            P("space", None),
            P("space", None),
        ),
        out_specs=P("mem", None, "space", None),
        check_vma=False,
    )
```

```python
import functools

import jax
import jax.numpy as jnp
from jax import lax
from jax.experimental import pallas as pl
from jax.experimental.pallas import tpu as pltpu
from jax.sharding import PartitionSpec as P

STEPS = 3
NS_ITERS = 6
GRAV = 1.0
DT = 0.3
VISC = 0.1
SUB = 4
HIGHEST = lax.Precision.HIGHEST
MESH = pl.DeviceIdType.MESH


def pieces(x):
    found = []
    for _ in range(3):
        part = x.astype(jnp.bfloat16)
        found.append(part)
        x = x - part.astype(jnp.float32)
    return found


def dot(a, b, contract=((1,), (0,))):
    def mul(x, y):
        return lax.dot_general(x, y, (contract, ((), ())), preferred_element_type=jnp.float32)

    a0, a1, a2 = pieces(a)
    b0, b1, b2 = pieces(b)
    small = (mul(a0, b2) + mul(a2, b0)) + mul(a1, b1)
    return (small + (mul(a0, b1) + mul(a1, b0))) + mul(a0, b0)


def kernel(
    dims,
    ens,
    depth,
    ocean_ref,
    cells,
    obs,
    out,
    state,
    fresh,
    hsend,
    hrecv,
    hot,
    split,
    picks,
    zpicks,
    mpicks,
    zobs,
    frecv,
    full,
    rback,
    h_ss,
    h_rs,
    o_ss,
    o_rs,
    z_ss,
    z_rs,
    m_ss,
    m_rs,
    f_ss,
    f_rs,
    b_ss,
    b_rs,
):
    n_mem, n_space, groups, gs, rows, cols, n_obs = dims
    members = n_mem * groups * gs
    padded = n_mem * groups * SUB
    per = rows * cols // n_mem
    i_mem = lax.axis_index("mem")
    i_space = lax.axis_index("space")

    barrier = pltpu.get_barrier_semaphore()
    for k in range(1, n_space):
        pl.semaphore_signal(
            barrier, inc=1, device_id={"space": lax.rem(i_space + k, n_space)}, device_id_type=MESH
        )
    for k in range(1, n_mem):
        pl.semaphore_signal(
            barrier, inc=1, device_id={"mem": lax.rem(i_mem + k, n_mem)}, device_id_type=MESH
        )
    pl.semaphore_wait(barrier, n_space - 1 + n_mem - 1)

    def remote(src, dst, ss, rs, where):
        return pltpu.make_async_remote_copy(
            src_ref=src, dst_ref=dst, send_sem=ss, recv_sem=rs, device_id=where, device_id_type=MESH
        )

    def to_space(k):
        return {"space": lax.rem(i_space + k, n_space)}

    def to_mem(k):
        return {"mem": lax.rem(i_mem + k, n_mem)}

    def nxt(x):
        return pltpu.roll(x, cols - 1, 1)

    def prv(x):
        return pltpu.roll(x, 1, 1)

    def north(x):
        return (nxt(x) - prv(x)) * 0.5

    coriolis = 0.05 + 0.1 * lax.broadcasted_iota(jnp.int32, (1, cols), 1).astype(jnp.float32) / cols
    half = DT * 0.5

    def get(step, g, field, r):
        if step == 0:
            return ens[g, field, r]
        return state[(step - 1) % 2, g, field, r]

    def total(step, g, r):
        return depth[pl.ds(r, 1), :] + get(step, g, 0, r)

    def halo_copies(step, g):
        found = []
        for d, k in ((0, n_space - 1), (1, 1)):
            found.append(
                remote(
                    hsend.at[step, g, d],
                    hrecv.at[step, g, d],
                    h_ss.at[step, g, d],
                    h_rs.at[step, g, d],
                    to_space(k),
                )
            )
        return found

    def send_edges(step, g):
        copies = halo_copies(step, g)
        for d, r, inner, sign in ((0, 0, 1, 1.0), (1, rows - 1, rows - 2, -1.0)):
            u, v = get(step, g, 1, r), get(step, g, 2, r)
            tot = total(step, g, r)
            inner_flux = total(step, g, inner) * get(step, g, 1, inner)
            hsend[step, g, d, 0] = u
            hsend[step, g, d, 1] = v
            hsend[step, g, d, 2] = tot * u
            hsend[step, g, d, 3] = get(step, g, 0, r) - (sign * half) * inner_flux - DT * north(tot * v)
            copies[d].start()

    def advance(step, g):
        for r in range(1, rows - 1):
            flux = [total(step, g, q) * get(step, g, 1, q) for q in (r - 1, r + 1)]
            fresh[r + 1] = (
                get(step, g, 0, r)
                - half * (flux[1] - flux[0])
                - DT * north(total(step, g, r) * get(step, g, 2, r))
            )
        copies = halo_copies(step, g)
        for d in (0, 1):
            copies[d].wait_recv()
        above, below = hrecv.at[step, g, 0], hrecv.at[step, g, 1]
        fresh[0] = below[3] - half * hsend[step, g, 0, 2]
        fresh[1] = hsend[step, g, 0, 3] + half * below[2]
        fresh[rows] = hsend[step, g, 1, 3] - half * above[2]
        fresh[rows + 1] = above[3] + half * hsend[step, g, 1, 2]

        def row(field, r):
            if r < 0:
                return below[field - 1]
            if r == rows:
                return above[field - 1]
            return get(step, g, field, r)

        slot = step % 2
        for r in range(rows):
            ocean = ocean_ref[pl.ds(r, 1), :]
            u, v = row(1, r), row(2, r)
            here = fresh[r + 1]
            state[slot, g, 0, r] = here
            for field, f, push, turn in (
                (1, u, (fresh[r + 2] - fresh[r]) * 0.5, -(coriolis * v)),
                (2, v, north(here), coriolis * u),
            ):
                up, down = row(field, r + 1), row(field, r - 1)
                right, left = nxt(f), prv(f)
                tend = GRAV * push + u * ((up - down) * 0.5) + v * ((right - left) * 0.5) + turn
                lap = up + down + right + left - 4.0 * f
                state[slot, g, field, r] = (f - DT * tend + DT * VISC * lap) * ocean

    last = (STEPS - 1) % 2

    def forward_copies(g):
        found = []
        for k in range(1, n_mem):
            first = lax.rem(i_mem + k, n_mem) * per
            found.append(
                remote(
                    state.at[last, g, :, first // cols, :, pl.ds(pl.multiple_of(lax.rem(first, cols), 128), per)],
                    frecv.at[g, k],
                    f_ss.at[g, k],
                    f_rs.at[g, k],
                    to_mem(k),
                )
            )
        return found

    obs_copies = [
        remote(obs, zobs.at[k], o_ss.at[k], o_rs.at[k], to_space(k)) for k in range(1, n_space)
    ]
    for g in range(groups):
        send_edges(0, g)
    for copy in obs_copies:
        copy.start()

    wanted = cells[...]
    for c in range(rows * cols // 128):
        index = lax.broadcasted_iota(jnp.int32, (128, n_obs), 0) + c * 128
        hot[pl.ds(c * 128, 128), :] = jnp.where(index == wanted, 1.0, 0.0).astype(jnp.bfloat16)
    split[...] = jnp.zeros_like(split)
    full[...] = jnp.zeros_like(full)

    for step in range(STEPS):
        for g in range(groups):
            advance(step, g)
            if step < STEPS - 1:
                send_edges(step + 1, g)
            else:
                for r in range(rows):
                    h = state[last, g, 0, r]
                    for p in range(3):
                        part = h.astype(jnp.bfloat16).astype(jnp.float32)
                        split[pl.ds((p * groups + g) * SUB, gs), pl.ds(r * cols, cols)] = part
                        h = h - part
                if g < groups - 1:
                    for copy in forward_copies(g):
                        copy.start()

    three = jnp.dot(split[...].astype(jnp.bfloat16), hot[...], preferred_element_type=jnp.float32)
    size = groups * SUB
    mine = three[:size] + three[size : 2 * size] + three[2 * size :]
    for g in range(groups):
        picks[g] = mine[g * SUB : g * SUB + gs]
        zpicks[0, g] = mine[g * SUB : g * SUB + gs]
    z_copies = [
        remote(picks, zpicks.at[k], z_ss.at[k], z_rs.at[k], to_space(k)) for k in range(1, n_space)
    ]
    for copy in z_copies:
        copy.start()
    for copy in z_copies:
        copy.wait_recv()
    m_copies = [
        remote(zpicks, mpicks.at[k], m_ss.at[k], m_rs.at[k], to_mem(k)) for k in range(1, n_mem)
    ]
    for copy in m_copies:
        copy.start()
    for copy in forward_copies(groups - 1):
        copy.start()
    for copy in obs_copies:
        copy.wait_recv()
    for copy in m_copies:
        copy.wait_recv()

    row_id = lax.broadcasted_iota(jnp.int32, (padded, n_obs), 0)
    valid = lax.rem(row_id, SUB) < gs
    gap = jnp.zeros((SUB - gs, n_obs), jnp.float32)
    gram = jnp.zeros((padded, padded), jnp.float32)
    drive = jnp.zeros((padded, 1), jnp.float32)
    for s in range(n_space):
        for k in range(n_mem):
            for g in range(groups):
                piece = zpicks[s, g] if k == 0 else mpicks[k, s, g]
                full[0, pl.ds((k * groups + g) * SUB, gs), pl.ds(0, n_obs)] = piece
        raw = full[0, :, pl.ds(0, n_obs)]
        hmean = jnp.sum(raw, axis=0, keepdims=True) / members
        values = obs[pl.ds(0, 1), :] if s == 0 else zobs[s, pl.ds(0, 1), :]
        errors = obs[pl.ds(1, 1), :] if s == 0 else zobs[s, pl.ds(1, 1), :]
        scaled = jnp.where(valid, (raw - hmean) / errors, 0.0)
        misfit = (values - hmean) / errors
        gram = gram + dot(scaled, scaled, ((1,), (1,)))
        drive = drive + jnp.sum(scaled * misfit, axis=1, keepdims=True)

    r_id = lax.broadcasted_iota(jnp.int32, (padded, padded), 0)
    c_id = lax.broadcasted_iota(jnp.int32, (padded, padded), 1)
    identity = jnp.where(r_id == c_id, 1.0, 0.0)
    system = identity + gram / (members - 1)
    squares = jnp.where(lax.rem(r_id, SUB) < gs, system * system, 0.0)
    norm_sq = jnp.sum(jnp.sum(squares, axis=1, keepdims=True), axis=0, keepdims=True)
    norm_scale = jnp.sqrt(norm_sq)
    iterate = system / norm_scale
    factor = 1.5 * identity - 0.5 * iterate
    carry = (dot(iterate, factor), factor)

    def sweep(_, carry):
        iterate, inverse = carry
        factor = 1.5 * identity - 0.5 * dot(inverse, iterate)
        return dot(iterate, factor), dot(factor, inverse)

    iterate, inverse = lax.fori_loop(0, NS_ITERS - 2, sweep, carry)
    factor = 1.5 * identity - 0.5 * dot(inverse, iterate)
    weights = dot(factor, inverse) / jnp.sqrt(norm_scale)
    once = jnp.sum(weights * drive, axis=0, keepdims=True)
    mean_weight = jnp.sum(weights * once, axis=1, keepdims=True) / (members - 1)
    mixing = (weights + mean_weight).T

    my_first = i_mem * per
    my_row = my_first // cols
    my_cols = pl.ds(pl.multiple_of(lax.rem(my_first, cols), 128), per)
    fwd = [forward_copies(g) for g in range(groups)]
    for g in range(groups):
        for f in range(3):
            full[f, pl.ds(g * SUB, gs), :] = state[last, g, f, my_row, :, my_cols]
        for k in range(1, n_mem):
            fwd[g][k - 1].wait_recv()
            for f in range(3):
                full[f, pl.ds((k * groups + g) * SUB, gs), :] = frecv[g, k, f]

    back = {}
    for g in range(groups):
        for k in range(1, n_mem):
            back[g, k] = remote(
                rback.at[g, k],
                out.at[g, :, my_row, :, my_cols],
                b_ss.at[g, k],
                b_rs.at[g, k],
                to_mem(n_mem - k),
            )
    for f in range(3):
        whole = full[f]
        center = jnp.sum(whole, axis=0, keepdims=True) / members
        done = center + dot(mixing, whole - center)
        for k in range(n_mem):
            for g in range(groups):
                piece = done[(k * groups + g) * SUB : (k * groups + g) * SUB + gs]
                if k == 0:
                    out[g, f, my_row, :, my_cols] = piece
                else:
                    rback[g, k, f] = piece
    for copy in back.values():
        copy.start()

    for step in range(STEPS):
        for g in range(groups):
            for copy in halo_copies(step, g):
                copy.wait_send()
    for copy in obs_copies + z_copies + m_copies + sum(fwd, []):
        copy.wait_send()
    for copy in back.values():
        copy.wait()


def local(ensemble, sea_depth, ocean_mask, observed_cells, observed_values, observed_error):
    n_mem = lax.axis_size("mem")
    n_space = lax.axis_size("space")
    local_members, fields, rows, cols = ensemble.shape
    n_obs = observed_cells.shape[1]
    gs = SUB if local_members % SUB == 0 else 1
    groups = local_members // gs
    per = rows * cols // n_mem
    padded = n_mem * groups * SUB
    dims = (n_mem, n_space, groups, gs, rows, cols, n_obs)
    ens = ensemble.reshape(groups, gs, fields, rows, cols).transpose(0, 2, 3, 1, 4)
    ocean = ocean_mask.astype(jnp.float32)
    obs = jnp.concatenate([observed_values, observed_error], axis=0)
    f32 = jnp.float32
    dma = pltpu.SemaphoreType.DMA
    result = pl.pallas_call(
        functools.partial(kernel, dims),
        out_shape=jax.ShapeDtypeStruct(ens.shape, f32),
        in_specs=[pl.BlockSpec(memory_space=pltpu.VMEM)] * 5,
        out_specs=pl.BlockSpec(memory_space=pltpu.VMEM),
        scratch_shapes=[
            pltpu.VMEM((2, groups, 3, rows, gs, cols), f32),
            pltpu.VMEM((rows + 2, gs, cols), f32),
            pltpu.VMEM((STEPS, groups, 2, 4, gs, cols), f32),
            pltpu.VMEM((STEPS, groups, 2, 4, gs, cols), f32),
            pltpu.VMEM((rows * cols, n_obs), jnp.bfloat16),
            pltpu.VMEM((3 * groups * SUB, rows * cols), f32),
            pltpu.VMEM((groups, gs, n_obs), f32),
            pltpu.VMEM((n_space, groups, gs, n_obs), f32),
            pltpu.VMEM((n_mem, n_space, groups, gs, n_obs), f32),
            pltpu.VMEM((n_space, 2, n_obs), f32),
            pltpu.VMEM((groups, n_mem, 3, gs, per), f32),
            pltpu.VMEM((3, padded, per), f32),
            pltpu.VMEM((groups, n_mem, 3, gs, per), f32),
            dma((STEPS, groups, 2)),
            dma((STEPS, groups, 2)),
            dma((n_space,)),
            dma((n_space,)),
            dma((n_space,)),
            dma((n_space,)),
            dma((n_mem,)),
            dma((n_mem,)),
            dma((groups, n_mem)),
            dma((groups, n_mem)),
            dma((groups, n_mem)),
            dma((groups, n_mem)),
        ],
        compiler_params=pltpu.CompilerParams(
            collective_id=0, has_side_effects=True, vmem_limit_bytes=48 * 1024 * 1024
        ),
    )(ens, sea_depth, ocean, observed_cells, obs)
    return result.transpose(0, 3, 1, 2, 4).reshape(ensemble.shape)


def solution(mesh):
    return jax.shard_map(
        local,
        mesh=mesh,
        in_specs=(
            P("mem", None, "space", None),
            P("space", None),
            P("space", None),
            P("space", None),
            P("space", None),
            P("space", None),
        ),
        out_specs=P("mem", None, "space", None),
        check_vma=False,
    )
```

```python
import functools

import jax
import jax.numpy as jnp
from jax import lax
from jax.experimental import pallas as pl
from jax.experimental.pallas import tpu as pltpu
from jax.sharding import PartitionSpec as P

STEPS = 3
NS_ITERS = 6
GRAV = 1.0
DT = 0.3
VISC = 0.1
SUB = 4
HIGHEST = lax.Precision.HIGHEST
MESH = pl.DeviceIdType.MESH


def pieces(x):
    found = []
    for _ in range(3):
        part = x.astype(jnp.bfloat16)
        found.append(part)
        x = x - part.astype(jnp.float32)
    return found


def dot(a, b, contract=((1,), (0,))):
    def mul(x, y):
        return lax.dot_general(x, y, (contract, ((), ())), preferred_element_type=jnp.float32)

    a0, a1, a2 = pieces(a)
    b0, b1, b2 = pieces(b)
    small = (mul(a0, b2) + mul(a2, b0)) + mul(a1, b1)
    return (small + (mul(a0, b1) + mul(a1, b0))) + mul(a0, b0)


def kernel(
    dims,
    ens,
    depth,
    ocean_ref,
    cells,
    values_ref,
    errors_ref,
    out,
    state,
    fresh,
    hsend,
    hrecv,
    hot,
    split,
    picks,
    zpicks,
    mpicks,
    obs,
    zobs,
    frecv,
    full,
    rback,
    h_ss,
    h_rs,
    o_ss,
    o_rs,
    z_ss,
    z_rs,
    m_ss,
    m_rs,
    f_ss,
    f_rs,
    b_ss,
    b_rs,
):
    n_mem, n_space, groups, gs, rows, cols, n_obs = dims
    members = n_mem * groups * gs
    padded = n_mem * groups * SUB
    per = rows * cols // n_mem
    i_mem = lax.axis_index("mem")
    i_space = lax.axis_index("space")

    barrier = pltpu.get_barrier_semaphore()
    for k in range(1, n_space):
        pl.semaphore_signal(
            barrier, inc=1, device_id={"space": lax.rem(i_space + k, n_space)}, device_id_type=MESH
        )
    for k in range(1, n_mem):
        pl.semaphore_signal(
            barrier, inc=1, device_id={"mem": lax.rem(i_mem + k, n_mem)}, device_id_type=MESH
        )
    pl.semaphore_wait(barrier, n_space - 1 + n_mem - 1)

    def remote(src, dst, ss, rs, where):
        return pltpu.make_async_remote_copy(
            src_ref=src, dst_ref=dst, send_sem=ss, recv_sem=rs, device_id=where, device_id_type=MESH
        )

    def to_space(k):
        return {"space": lax.rem(i_space + k, n_space)}

    def to_mem(k):
        return {"mem": lax.rem(i_mem + k, n_mem)}

    def nxt(x):
        return pltpu.roll(x, cols - 1, 1)

    def prv(x):
        return pltpu.roll(x, 1, 1)

    def north(x):
        return (nxt(x) - prv(x)) * 0.5

    coriolis = 0.05 + 0.1 * lax.broadcasted_iota(jnp.int32, (1, cols), 1).astype(jnp.float32) / cols
    half = DT * 0.5

    def get(step, g, field, r):
        if step == 0:
            return ens[g, field, r]
        return state[(step - 1) % 2, g, field, r]

    def total(step, g, r):
        return depth[pl.ds(r, 1), :] + get(step, g, 0, r)

    def halo_copies(step, g):
        found = []
        for d, k in ((0, n_space - 1), (1, 1)):
            found.append(
                remote(
                    hsend.at[step, g, d],
                    hrecv.at[step, g, d],
                    h_ss.at[step, g, d],
                    h_rs.at[step, g, d],
                    to_space(k),
                )
            )
        return found

    def send_edges(step, g):
        copies = halo_copies(step, g)
        for d, r, inner, sign in ((0, 0, 1, 1.0), (1, rows - 1, rows - 2, -1.0)):
            u, v = get(step, g, 1, r), get(step, g, 2, r)
            tot = total(step, g, r)
            inner_flux = total(step, g, inner) * get(step, g, 1, inner)
            hsend[step, g, d, 0] = u
            hsend[step, g, d, 1] = v
            hsend[step, g, d, 2] = tot * u
            hsend[step, g, d, 3] = get(step, g, 0, r) - (sign * half) * inner_flux - DT * north(tot * v)
            copies[d].start()

    def advance(step, g):
        for r in range(1, rows - 1):
            flux = [total(step, g, q) * get(step, g, 1, q) for q in (r - 1, r + 1)]
            fresh[r + 1] = (
                get(step, g, 0, r)
                - half * (flux[1] - flux[0])
                - DT * north(total(step, g, r) * get(step, g, 2, r))
            )
        copies = halo_copies(step, g)
        for d in (0, 1):
            copies[d].wait_recv()
        above, below = hrecv.at[step, g, 0], hrecv.at[step, g, 1]
        fresh[0] = below[3] - half * hsend[step, g, 0, 2]
        fresh[1] = hsend[step, g, 0, 3] + half * below[2]
        fresh[rows] = hsend[step, g, 1, 3] - half * above[2]
        fresh[rows + 1] = above[3] + half * hsend[step, g, 1, 2]

        def row(field, r):
            if r < 0:
                return below[field - 1]
            if r == rows:
                return above[field - 1]
            return get(step, g, field, r)

        slot = step % 2
        for r in range(rows):
            ocean = ocean_ref[pl.ds(r, 1), :].astype(jnp.float32)
            u, v = row(1, r), row(2, r)
            here = fresh[r + 1]
            state[slot, g, 0, r] = here
            for field, f, push, turn in (
                (1, u, (fresh[r + 2] - fresh[r]) * 0.5, -(coriolis * v)),
                (2, v, north(here), coriolis * u),
            ):
                up, down = row(field, r + 1), row(field, r - 1)
                right, left = nxt(f), prv(f)
                tend = GRAV * push + u * ((up - down) * 0.5) + v * ((right - left) * 0.5) + turn
                lap = up + down + right + left - 4.0 * f
                state[slot, g, field, r] = (f - DT * tend + DT * VISC * lap) * ocean

    last = (STEPS - 1) % 2

    def forward_copies(g):
        found = []
        for k in range(1, n_mem):
            first = lax.rem(i_mem + k, n_mem) * per
            found.append(
                remote(
                    state.at[last, g, :, first // cols, :, pl.ds(pl.multiple_of(lax.rem(first, cols), 128), per)],
                    frecv.at[g, k],
                    f_ss.at[g, k],
                    f_rs.at[g, k],
                    to_mem(k),
                )
            )
        return found

    obs[pl.ds(0, 1), :] = values_ref[...]
    obs[pl.ds(1, 1), :] = errors_ref[...]
    obs_copies = [
        remote(obs, zobs.at[k], o_ss.at[k], o_rs.at[k], to_space(k)) for k in range(1, n_space)
    ]
    for g in range(groups):
        send_edges(0, g)
    for copy in obs_copies:
        copy.start()

    wanted = cells[...]
    for c in range(rows * cols // 128):
        index = lax.broadcasted_iota(jnp.int32, (128, n_obs), 0) + c * 128
        hot[pl.ds(c * 128, 128), :] = jnp.where(index == wanted, 1.0, 0.0).astype(jnp.bfloat16)
    split[...] = jnp.zeros_like(split)
    full[...] = jnp.zeros_like(full)

    for step in range(STEPS):
        for g in range(groups):
            advance(step, g)
            if step < STEPS - 1:
                send_edges(step + 1, g)
            else:
                for r in range(rows):
                    h = state[last, g, 0, r]
                    for p in range(3):
                        part = h.astype(jnp.bfloat16).astype(jnp.float32)
                        split[pl.ds((p * groups + g) * SUB, gs), pl.ds(r * cols, cols)] = part
                        h = h - part
                if g < groups - 1:
                    for copy in forward_copies(g):
                        copy.start()

    three = jnp.dot(split[...].astype(jnp.bfloat16), hot[...], preferred_element_type=jnp.float32)
    size = groups * SUB
    mine = three[:size] + three[size : 2 * size] + three[2 * size :]
    for g in range(groups):
        picks[g] = mine[g * SUB : g * SUB + gs]
        zpicks[0, g] = mine[g * SUB : g * SUB + gs]
    z_copies = [
        remote(picks, zpicks.at[k], z_ss.at[k], z_rs.at[k], to_space(k)) for k in range(1, n_space)
    ]
    for copy in z_copies:
        copy.start()
    for copy in z_copies:
        copy.wait_recv()
    m_copies = [
        remote(zpicks, mpicks.at[k], m_ss.at[k], m_rs.at[k], to_mem(k)) for k in range(1, n_mem)
    ]
    for copy in m_copies:
        copy.start()
    for copy in forward_copies(groups - 1):
        copy.start()
    for copy in obs_copies:
        copy.wait_recv()
    for copy in m_copies:
        copy.wait_recv()

    row_id = lax.broadcasted_iota(jnp.int32, (padded, n_obs), 0)
    valid = lax.rem(row_id, SUB) < gs
    gram = jnp.zeros((padded, padded), jnp.float32)
    drive = jnp.zeros((padded, 1), jnp.float32)
    for s in range(n_space):
        for k in range(n_mem):
            for g in range(groups):
                piece = zpicks[s, g] if k == 0 else mpicks[k, s, g]
                full[0, pl.ds((k * groups + g) * SUB, gs), pl.ds(0, n_obs)] = piece
        raw = full[0, :, pl.ds(0, n_obs)]
        hmean = jnp.sum(raw, axis=0, keepdims=True) / members
        values = obs[pl.ds(0, 1), :] if s == 0 else zobs[s, pl.ds(0, 1), :]
        errors = obs[pl.ds(1, 1), :] if s == 0 else zobs[s, pl.ds(1, 1), :]
        scaled = jnp.where(valid, (raw - hmean) / errors, 0.0)
        misfit = (values - hmean) / errors
        gram = gram + dot(scaled, scaled, ((1,), (1,)))
        drive = drive + jnp.sum(scaled * misfit, axis=1, keepdims=True)

    r_id = lax.broadcasted_iota(jnp.int32, (padded, padded), 0)
    c_id = lax.broadcasted_iota(jnp.int32, (padded, padded), 1)
    identity = jnp.where(r_id == c_id, 1.0, 0.0)
    system = identity + gram / (members - 1)
    squares = jnp.where(lax.rem(r_id, SUB) < gs, system * system, 0.0)
    norm_sq = jnp.sum(jnp.sum(squares, axis=1, keepdims=True), axis=0, keepdims=True)
    norm_scale = jnp.sqrt(norm_sq)
    iterate = system / norm_scale
    factor = 1.5 * identity - 0.5 * iterate
    carry = (dot(iterate, factor), factor)

    def sweep(_, carry):
        iterate, inverse = carry
        factor = 1.5 * identity - 0.5 * dot(inverse, iterate)
        return dot(iterate, factor), dot(factor, inverse)

    iterate, inverse = lax.fori_loop(0, NS_ITERS - 2, sweep, carry)
    factor = 1.5 * identity - 0.5 * dot(inverse, iterate)
    weights = dot(factor, inverse) / jnp.sqrt(norm_scale)
    once = jnp.sum(weights * drive, axis=0, keepdims=True)
    mean_weight = jnp.sum(weights * once, axis=1, keepdims=True) / (members - 1)
    mixing = (weights + mean_weight).T

    my_first = i_mem * per
    my_row = my_first // cols
    my_cols = pl.ds(pl.multiple_of(lax.rem(my_first, cols), 128), per)
    fwd = [forward_copies(g) for g in range(groups)]
    for g in range(groups):
        for f in range(3):
            full[f, pl.ds(g * SUB, gs), :] = state[last, g, f, my_row, :, my_cols]
        for k in range(1, n_mem):
            fwd[g][k - 1].wait_recv()
            for f in range(3):
                full[f, pl.ds((k * groups + g) * SUB, gs), :] = frecv[g, k, f]

    back = []
    for f in range(3):
        whole = full[f]
        center = jnp.sum(whole, axis=0, keepdims=True) / members
        done = center + dot(mixing, whole - center)
        for k in range(n_mem):
            for g in range(groups):
                piece = done[(k * groups + g) * SUB : (k * groups + g) * SUB + gs]
                if k == 0:
                    out[g, f, my_row, :, my_cols] = piece
                else:
                    rback[k, f, g] = piece
        for k in range(1, n_mem):
            copy = remote(
                rback.at[k, f],
                out.at[:, f, my_row, :, my_cols],
                b_ss.at[k, f],
                b_rs.at[k, f],
                to_mem(n_mem - k),
            )
            copy.start()
            back.append(copy)

    for step in range(STEPS):
        for g in range(groups):
            for copy in halo_copies(step, g):
                copy.wait_send()
    for copy in obs_copies + z_copies + m_copies + sum(fwd, []):
        copy.wait_send()
    for copy in back:
        copy.wait()


def local(ensemble, sea_depth, ocean_mask, observed_cells, observed_values, observed_error):
    n_mem = lax.axis_size("mem")
    n_space = lax.axis_size("space")
    local_members, fields, rows, cols = ensemble.shape
    n_obs = observed_cells.shape[1]
    gs = SUB if local_members % SUB == 0 else 1
    groups = local_members // gs
    per = rows * cols // n_mem
    padded = n_mem * groups * SUB
    dims = (n_mem, n_space, groups, gs, rows, cols, n_obs)
    ens = ensemble.reshape(groups, gs, fields, rows, cols).transpose(0, 2, 3, 1, 4)
    f32 = jnp.float32
    dma = pltpu.SemaphoreType.DMA
    result = pl.pallas_call(
        functools.partial(kernel, dims),
        out_shape=jax.ShapeDtypeStruct(ens.shape, f32),
        in_specs=[pl.BlockSpec(memory_space=pltpu.VMEM)] * 6,
        out_specs=pl.BlockSpec(memory_space=pltpu.VMEM),
        scratch_shapes=[
            pltpu.VMEM((2, groups, 3, rows, gs, cols), f32),
            pltpu.VMEM((rows + 2, gs, cols), f32),
            pltpu.VMEM((STEPS, groups, 2, 4, gs, cols), f32),
            pltpu.VMEM((STEPS, groups, 2, 4, gs, cols), f32),
            pltpu.VMEM((rows * cols, n_obs), jnp.bfloat16),
            pltpu.VMEM((3 * groups * SUB, rows * cols), f32),
            pltpu.VMEM((groups, gs, n_obs), f32),
            pltpu.VMEM((n_space, groups, gs, n_obs), f32),
            pltpu.VMEM((n_mem, n_space, groups, gs, n_obs), f32),
            pltpu.VMEM((2, n_obs), f32),
            pltpu.VMEM((n_space, 2, n_obs), f32),
            pltpu.VMEM((groups, n_mem, 3, gs, per), f32),
            pltpu.VMEM((3, padded, per), f32),
            pltpu.VMEM((n_mem, 3, groups, gs, per), f32),
            dma((STEPS, groups, 2)),
            dma((STEPS, groups, 2)),
            dma((n_space,)),
            dma((n_space,)),
            dma((n_space,)),
            dma((n_space,)),
            dma((n_mem,)),
            dma((n_mem,)),
            dma((groups, n_mem)),
            dma((groups, n_mem)),
            dma((n_mem, 3)),
            dma((n_mem, 3)),
        ],
        compiler_params=pltpu.CompilerParams(
            collective_id=0, has_side_effects=True, vmem_limit_bytes=48 * 1024 * 1024
        ),
    )(ens, sea_depth, ocean_mask, observed_cells, observed_values, observed_error)
    return result.transpose(0, 3, 1, 2, 4).reshape(ensemble.shape)


def solution(mesh):
    return jax.shard_map(
        local,
        mesh=mesh,
        in_specs=(
            P("mem", None, "space", None),
            P("space", None),
            P("space", None),
            P("space", None),
            P("space", None),
            P("space", None),
        ),
        out_specs=P("mem", None, "space", None),
        check_vma=False,
    )
```

```python
import functools

import jax
import jax.numpy as jnp
from jax import lax
from jax.experimental import pallas as pl
from jax.experimental.pallas import tpu as pltpu
from jax.sharding import PartitionSpec as P

STEPS = 3
NS_ITERS = 6
GRAV = 1.0
DT = 0.3
VISC = 0.1
SUB = 4
HIGHEST = lax.Precision.HIGHEST
MESH = pl.DeviceIdType.MESH


def pieces(x):
    found = []
    for _ in range(3):
        part = x.astype(jnp.bfloat16)
        found.append(part)
        x = x - part.astype(jnp.float32)
    return found


def dot(a, b, contract=((1,), (0,))):
    def mul(x, y):
        return lax.dot_general(x, y, (contract, ((), ())), preferred_element_type=jnp.float32)

    a0, a1, a2 = pieces(a)
    b0, b1, b2 = pieces(b)
    small = (mul(a0, b2) + mul(a2, b0)) + mul(a1, b1)
    return (small + (mul(a0, b1) + mul(a1, b0))) + mul(a0, b0)


def kernel(
    dims,
    ens,
    depth,
    ocean_ref,
    cells,
    values_ref,
    errors_ref,
    out,
    state,
    fresh,
    hsend,
    hrecv,
    hot,
    split,
    picks,
    zpicks,
    mpicks,
    obs,
    zobs,
    frecv,
    full,
    xall,
    rback,
    h_ss,
    h_rs,
    o_ss,
    o_rs,
    z_ss,
    z_rs,
    m_ss,
    m_rs,
    f_ss,
    f_rs,
    b_ss,
    b_rs,
):
    n_mem, n_space, groups, gs, rows, cols, n_obs = dims
    members = n_mem * groups * gs
    padded = n_mem * groups * SUB
    per = rows * cols // n_mem
    i_mem = lax.axis_index("mem")
    i_space = lax.axis_index("space")

    barrier = pltpu.get_barrier_semaphore()
    for k in range(1, n_space):
        pl.semaphore_signal(
            barrier, inc=1, device_id={"space": lax.rem(i_space + k, n_space)}, device_id_type=MESH
        )
    for k in range(1, n_mem):
        pl.semaphore_signal(
            barrier, inc=1, device_id={"mem": lax.rem(i_mem + k, n_mem)}, device_id_type=MESH
        )
    pl.semaphore_wait(barrier, n_space - 1 + n_mem - 1)

    def remote(src, dst, ss, rs, where):
        return pltpu.make_async_remote_copy(
            src_ref=src, dst_ref=dst, send_sem=ss, recv_sem=rs, device_id=where, device_id_type=MESH
        )

    def to_space(k):
        return {"space": lax.rem(i_space + k, n_space)}

    def to_mem(k):
        return {"mem": lax.rem(i_mem + k, n_mem)}

    def nxt(x):
        return pltpu.roll(x, cols - 1, 1)

    def prv(x):
        return pltpu.roll(x, 1, 1)

    def north(x):
        return (nxt(x) - prv(x)) * 0.5

    coriolis = 0.05 + 0.1 * lax.broadcasted_iota(jnp.int32, (1, cols), 1).astype(jnp.float32) / cols
    half = DT * 0.5

    def get(step, g, field, r):
        if step == 0:
            return ens[g, field, r]
        return state[(step - 1) % 2, g, field, r]

    def total(step, g, r):
        return depth[pl.ds(r, 1), :] + get(step, g, 0, r)

    def halo_copies(step, g):
        found = []
        for d, k in ((0, n_space - 1), (1, 1)):
            found.append(
                remote(
                    hsend.at[step, g, d],
                    hrecv.at[step, g, d],
                    h_ss.at[step, g, d],
                    h_rs.at[step, g, d],
                    to_space(k),
                )
            )
        return found

    def send_edges(step, g):
        copies = halo_copies(step, g)
        for d, r, inner, sign in ((0, 0, 1, 1.0), (1, rows - 1, rows - 2, -1.0)):
            u, v = get(step, g, 1, r), get(step, g, 2, r)
            tot = total(step, g, r)
            inner_flux = total(step, g, inner) * get(step, g, 1, inner)
            hsend[step, g, d, 0] = u
            hsend[step, g, d, 1] = v
            hsend[step, g, d, 2] = tot * u
            hsend[step, g, d, 3] = get(step, g, 0, r) - (sign * half) * inner_flux - DT * north(tot * v)
            copies[d].start()

    def advance(step, g):
        for r in range(1, rows - 1):
            flux = [total(step, g, q) * get(step, g, 1, q) for q in (r - 1, r + 1)]
            fresh[r + 1] = (
                get(step, g, 0, r)
                - half * (flux[1] - flux[0])
                - DT * north(total(step, g, r) * get(step, g, 2, r))
            )
        copies = halo_copies(step, g)
        for d in (0, 1):
            copies[d].wait_recv()
        above, below = hrecv.at[step, g, 0], hrecv.at[step, g, 1]
        fresh[0] = below[3] - half * hsend[step, g, 0, 2]
        fresh[1] = hsend[step, g, 0, 3] + half * below[2]
        fresh[rows] = hsend[step, g, 1, 3] - half * above[2]
        fresh[rows + 1] = above[3] + half * hsend[step, g, 1, 2]

        def row(field, r):
            if r < 0:
                return below[field - 1]
            if r == rows:
                return above[field - 1]
            return get(step, g, field, r)

        slot = step % 2
        for r in range(rows):
            ocean = ocean_ref[pl.ds(r, 1), :].astype(jnp.float32)
            u, v = row(1, r), row(2, r)
            here = fresh[r + 1]
            state[slot, g, 0, r] = here
            for field, f, push, turn in (
                (1, u, (fresh[r + 2] - fresh[r]) * 0.5, -(coriolis * v)),
                (2, v, north(here), coriolis * u),
            ):
                up, down = row(field, r + 1), row(field, r - 1)
                right, left = nxt(f), prv(f)
                tend = GRAV * push + u * ((up - down) * 0.5) + v * ((right - left) * 0.5) + turn
                lap = up + down + right + left - 4.0 * f
                state[slot, g, field, r] = (f - DT * tend + DT * VISC * lap) * ocean

    last = (STEPS - 1) % 2

    def forward_copies(g):
        found = []
        for k in range(1, n_mem):
            first = lax.rem(i_mem + k, n_mem) * per
            found.append(
                remote(
                    state.at[last, g, :, first // cols, :, pl.ds(pl.multiple_of(lax.rem(first, cols), 128), per)],
                    frecv.at[g, k],
                    f_ss.at[g, k],
                    f_rs.at[g, k],
                    to_mem(k),
                )
            )
        return found

    obs[pl.ds(0, 1), :] = values_ref[...]
    obs[pl.ds(1, 1), :] = errors_ref[...]
    obs_copies = [
        remote(obs, zobs.at[k], o_ss.at[k], o_rs.at[k], to_space(k)) for k in range(1, n_space)
    ]
    for g in range(groups):
        send_edges(0, g)
    for copy in obs_copies:
        copy.start()

    wanted = cells[...]
    for c in range(rows * cols // 128):
        index = lax.broadcasted_iota(jnp.int32, (128, n_obs), 0) + c * 128
        hot[pl.ds(c * 128, 128), :] = jnp.where(index == wanted, 1.0, 0.0).astype(jnp.bfloat16)
    split[...] = jnp.zeros_like(split)
    full[...] = jnp.zeros_like(full)
    xall[...] = jnp.zeros_like(xall)

    for step in range(STEPS):
        for g in range(groups):
            advance(step, g)
            if step < STEPS - 1:
                send_edges(step + 1, g)
            else:
                for r in range(rows):
                    h = state[last, g, 0, r]
                    for p in range(3):
                        part = h.astype(jnp.bfloat16).astype(jnp.float32)
                        split[pl.ds((p * groups + g) * SUB, gs), pl.ds(r * cols, cols)] = part
                        h = h - part
                if g < groups - 1:
                    for copy in forward_copies(g):
                        copy.start()

    three = jnp.dot(split[...].astype(jnp.bfloat16), hot[...], preferred_element_type=jnp.float32)
    size = groups * SUB
    mine = three[:size] + three[size : 2 * size] + three[2 * size :]
    for g in range(groups):
        picks[g] = mine[g * SUB : g * SUB + gs]
        zpicks[0, g] = mine[g * SUB : g * SUB + gs]
    z_copies = [
        remote(picks, zpicks.at[k], z_ss.at[k], z_rs.at[k], to_space(k)) for k in range(1, n_space)
    ]
    for copy in z_copies:
        copy.start()
    for copy in z_copies:
        copy.wait_recv()
    m_copies = [
        remote(zpicks, mpicks.at[k], m_ss.at[k], m_rs.at[k], to_mem(k)) for k in range(1, n_mem)
    ]
    for copy in m_copies:
        copy.start()
    for copy in forward_copies(groups - 1):
        copy.start()
    my_first = i_mem * per
    my_row = my_first // cols
    my_cols = pl.ds(pl.multiple_of(lax.rem(my_first, cols), 128), per)
    fwd = [forward_copies(g) for g in range(groups)]

    def collect(g):
        for f in range(3):
            full[f, pl.ds(g * SUB, gs), :] = state[last, g, f, my_row, :, my_cols]
        for k in range(1, n_mem):
            fwd[g][k - 1].wait_recv()
            for f in range(3):
                full[f, pl.ds((k * groups + g) * SUB, gs), :] = frecv[g, k, f]

    for g in range(groups - 1):
        collect(g)
    for copy in obs_copies:
        copy.wait_recv()
    for k in range(n_mem):
        if k > 0:
            m_copies[k - 1].wait_recv()
        for s in range(n_space):
            for g in range(groups):
                piece = zpicks[s, g] if k == 0 else mpicks[k, s, g]
                xall[pl.ds((k * groups + g) * SUB, gs), pl.ds(s * n_obs, n_obs)] = piece

    all_obs = [obs[...]] + [zobs[s] for s in range(1, n_space)]
    values = jnp.concatenate([pair[0:1] for pair in all_obs], axis=1)
    errors = jnp.concatenate([pair[1:2] for pair in all_obs], axis=1)
    valid = lax.rem(lax.broadcasted_iota(jnp.int32, (padded, n_space * n_obs), 0), SUB) < gs
    raw = xall[...]
    hmean = jnp.sum(raw, axis=0, keepdims=True) / members
    scaled = jnp.where(valid, (raw - hmean) / errors, 0.0)
    misfit = (values - hmean) / errors
    gram = dot(scaled, scaled, ((1,), (1,)))
    drive = jnp.sum(scaled * misfit, axis=1, keepdims=True)

    r_id = lax.broadcasted_iota(jnp.int32, (padded, padded), 0)
    c_id = lax.broadcasted_iota(jnp.int32, (padded, padded), 1)
    identity = jnp.where(r_id == c_id, 1.0, 0.0)
    system = identity + gram / (members - 1)
    squares = jnp.where(lax.rem(r_id, SUB) < gs, system * system, 0.0)
    norm_sq = jnp.sum(jnp.sum(squares, axis=1, keepdims=True), axis=0, keepdims=True)
    norm_scale = jnp.sqrt(norm_sq)
    iterate = system / norm_scale
    factor = 1.5 * identity - 0.5 * iterate
    carry = (dot(iterate, factor), factor)

    def sweep(_, carry):
        iterate, inverse = carry
        factor = 1.5 * identity - 0.5 * dot(inverse, iterate)
        return dot(iterate, factor), dot(factor, inverse)

    iterate, inverse = lax.fori_loop(0, NS_ITERS - 2, sweep, carry)
    factor = 1.5 * identity - 0.5 * dot(inverse, iterate)
    weights = dot(factor, inverse) / jnp.sqrt(norm_scale)
    once = jnp.sum(weights * drive, axis=0, keepdims=True)
    mean_weight = jnp.sum(weights * once, axis=1, keepdims=True) / (members - 1)
    mixing = (weights + mean_weight).T

    collect(groups - 1)

    back = []
    for f in range(3):
        whole = full[f]
        center = jnp.sum(whole, axis=0, keepdims=True) / members
        done = center + dot(mixing, whole - center)
        for k in range(n_mem):
            for g in range(groups):
                piece = done[(k * groups + g) * SUB : (k * groups + g) * SUB + gs]
                if k == 0:
                    out[g, f, my_row, :, my_cols] = piece
                else:
                    rback[k, f, g] = piece
        for k in range(1, n_mem):
            copy = remote(
                rback.at[k, f],
                out.at[:, f, my_row, :, my_cols],
                b_ss.at[k, f],
                b_rs.at[k, f],
                to_mem(n_mem - k),
            )
            copy.start()
            back.append(copy)

    for step in range(STEPS):
        for g in range(groups):
            for copy in halo_copies(step, g):
                copy.wait_send()
    for copy in obs_copies + z_copies + m_copies + sum(fwd, []):
        copy.wait_send()
    for copy in back:
        copy.wait()


def local(ensemble, sea_depth, ocean_mask, observed_cells, observed_values, observed_error):
    n_mem = lax.axis_size("mem")
    n_space = lax.axis_size("space")
    local_members, fields, rows, cols = ensemble.shape
    n_obs = observed_cells.shape[1]
    gs = SUB if local_members % SUB == 0 else 1
    groups = local_members // gs
    per = rows * cols // n_mem
    padded = n_mem * groups * SUB
    dims = (n_mem, n_space, groups, gs, rows, cols, n_obs)
    ens = ensemble.reshape(groups, gs, fields, rows, cols).transpose(0, 2, 3, 1, 4)
    f32 = jnp.float32
    dma = pltpu.SemaphoreType.DMA
    result = pl.pallas_call(
        functools.partial(kernel, dims),
        out_shape=jax.ShapeDtypeStruct(ens.shape, f32),
        in_specs=[pl.BlockSpec(memory_space=pltpu.VMEM)] * 6,
        out_specs=pl.BlockSpec(memory_space=pltpu.VMEM),
        scratch_shapes=[
            pltpu.VMEM((2, groups, 3, rows, gs, cols), f32),
            pltpu.VMEM((rows + 2, gs, cols), f32),
            pltpu.VMEM((STEPS, groups, 2, 4, gs, cols), f32),
            pltpu.VMEM((STEPS, groups, 2, 4, gs, cols), f32),
            pltpu.VMEM((rows * cols, n_obs), jnp.bfloat16),
            pltpu.VMEM((3 * groups * SUB, rows * cols), f32),
            pltpu.VMEM((groups, gs, n_obs), f32),
            pltpu.VMEM((n_space, groups, gs, n_obs), f32),
            pltpu.VMEM((n_mem, n_space, groups, gs, n_obs), f32),
            pltpu.VMEM((2, n_obs), f32),
            pltpu.VMEM((n_space, 2, n_obs), f32),
            pltpu.VMEM((groups, n_mem, 3, gs, per), f32),
            pltpu.VMEM((3, padded, per), f32),
            pltpu.VMEM((padded, n_space * n_obs), f32),
            pltpu.VMEM((n_mem, 3, groups, gs, per), f32),
            dma((STEPS, groups, 2)),
            dma((STEPS, groups, 2)),
            dma((n_space,)),
            dma((n_space,)),
            dma((n_space,)),
            dma((n_space,)),
            dma((n_mem,)),
            dma((n_mem,)),
            dma((groups, n_mem)),
            dma((groups, n_mem)),
            dma((n_mem, 3)),
            dma((n_mem, 3)),
        ],
        compiler_params=pltpu.CompilerParams(
            collective_id=0, has_side_effects=True, vmem_limit_bytes=48 * 1024 * 1024
        ),
    )(ens, sea_depth, ocean_mask, observed_cells, observed_values, observed_error)
    return result.transpose(0, 3, 1, 2, 4).reshape(ensemble.shape)


def solution(mesh):
    return jax.shard_map(
        local,
        mesh=mesh,
        in_specs=(
            P("mem", None, "space", None),
            P("space", None),
            P("space", None),
            P("space", None),
            P("space", None),
            P("space", None),
        ),
        out_specs=P("mem", None, "space", None),
        check_vma=False,
    )
```

```python
import functools

import jax
import jax.numpy as jnp
from jax import lax
from jax.experimental import pallas as pl
from jax.experimental.pallas import tpu as pltpu
from jax.sharding import PartitionSpec as P

STEPS = 3
NS_ITERS = 6
GRAV = 1.0
DT = 0.3
VISC = 0.1
SUB = 4
HIGHEST = lax.Precision.HIGHEST
MESH = pl.DeviceIdType.MESH


def pieces(x):
    found = []
    for _ in range(3):
        part = x.astype(jnp.bfloat16)
        found.append(part)
        x = x - part.astype(jnp.float32)
    return found


def dot(a, b, contract=((1,), (0,))):
    def mul(x, y):
        return lax.dot_general(x, y, (contract, ((), ())), preferred_element_type=jnp.float32)

    a0, a1, a2 = pieces(a)
    b0, b1, b2 = pieces(b)
    small = (mul(a0, b2) + mul(a2, b0)) + mul(a1, b1)
    return (small + (mul(a0, b1) + mul(a1, b0))) + mul(a0, b0)


def kernel(
    dims,
    ens,
    depth,
    ocean_ref,
    cells,
    values_ref,
    errors_ref,
    out,
    state,
    fresh,
    hsend,
    hrecv,
    hot,
    split,
    picks,
    zpicks,
    mpicks,
    obs,
    zobs,
    frecv,
    full,
    xall,
    rback,
    h_ss,
    h_rs,
    o_ss,
    o_rs,
    z_ss,
    z_rs,
    m_ss,
    m_rs,
    f_ss,
    f_rs,
    b_ss,
    b_rs,
):
    n_mem, n_space, groups, gs, rows, cols, n_obs = dims
    members = n_mem * groups * gs
    padded = n_mem * groups * SUB
    per = rows * cols // n_mem
    i_mem = lax.axis_index("mem")
    i_space = lax.axis_index("space")

    barrier = pltpu.get_barrier_semaphore()
    for k in range(1, n_space):
        pl.semaphore_signal(
            barrier, inc=1, device_id={"space": lax.rem(i_space + k, n_space)}, device_id_type=MESH
        )
    for k in range(1, n_mem):
        pl.semaphore_signal(
            barrier, inc=1, device_id={"mem": lax.rem(i_mem + k, n_mem)}, device_id_type=MESH
        )
    pl.semaphore_wait(barrier, n_space - 1 + n_mem - 1)

    def remote(src, dst, ss, rs, where):
        return pltpu.make_async_remote_copy(
            src_ref=src, dst_ref=dst, send_sem=ss, recv_sem=rs, device_id=where, device_id_type=MESH
        )

    def to_space(k):
        return {"space": lax.rem(i_space + k, n_space)}

    def to_mem(k):
        return {"mem": lax.rem(i_mem + k, n_mem)}

    def nxt(x):
        return pltpu.roll(x, cols - 1, 1)

    def prv(x):
        return pltpu.roll(x, 1, 1)

    def north(x):
        return (nxt(x) - prv(x)) * 0.5

    coriolis = 0.05 + 0.1 * lax.broadcasted_iota(jnp.int32, (1, cols), 1).astype(jnp.float32) / cols
    half = DT * 0.5

    def get(step, g, field, r):
        if step == 0:
            return ens[g, field, r]
        return state[(step - 1) % 2, g, field, r]

    def total(step, g, r):
        return depth[pl.ds(r, 1), :] + get(step, g, 0, r)

    def halo_copies(step, g):
        found = []
        for d, k in ((0, n_space - 1), (1, 1)):
            found.append(
                remote(
                    hsend.at[step, g, d],
                    hrecv.at[step, g, d],
                    h_ss.at[step, g, d],
                    h_rs.at[step, g, d],
                    to_space(k),
                )
            )
        return found

    def send_edges(step, g):
        copies = halo_copies(step, g)
        for d, r, inner, sign in ((0, 0, 1, 1.0), (1, rows - 1, rows - 2, -1.0)):
            u, v = get(step, g, 1, r), get(step, g, 2, r)
            tot = total(step, g, r)
            inner_flux = total(step, g, inner) * get(step, g, 1, inner)
            hsend[step, g, d, 0] = u
            hsend[step, g, d, 1] = v
            hsend[step, g, d, 2] = tot * u
            hsend[step, g, d, 3] = get(step, g, 0, r) - (sign * half) * inner_flux - DT * north(tot * v)
            copies[d].start()

    def advance(step, g):
        for r in range(1, rows - 1):
            flux = [total(step, g, q) * get(step, g, 1, q) for q in (r - 1, r + 1)]
            fresh[r + 1] = (
                get(step, g, 0, r)
                - half * (flux[1] - flux[0])
                - DT * north(total(step, g, r) * get(step, g, 2, r))
            )
        copies = halo_copies(step, g)
        for d in (0, 1):
            copies[d].wait_recv()
        above, below = hrecv.at[step, g, 0], hrecv.at[step, g, 1]
        fresh[0] = below[3] - half * hsend[step, g, 0, 2]
        fresh[1] = hsend[step, g, 0, 3] + half * below[2]
        fresh[rows] = hsend[step, g, 1, 3] - half * above[2]
        fresh[rows + 1] = above[3] + half * hsend[step, g, 1, 2]

        def row(field, r):
            if r < 0:
                return below[field - 1]
            if r == rows:
                return above[field - 1]
            return get(step, g, field, r)

        slot = step % 2
        for r in range(rows):
            ocean = ocean_ref[pl.ds(r, 1), :].astype(jnp.float32)
            u, v = row(1, r), row(2, r)
            here = fresh[r + 1]
            state[slot, g, 0, r] = here
            for field, f, push, turn in (
                (1, u, (fresh[r + 2] - fresh[r]) * 0.5, -(coriolis * v)),
                (2, v, north(here), coriolis * u),
            ):
                up, down = row(field, r + 1), row(field, r - 1)
                right, left = nxt(f), prv(f)
                tend = GRAV * push + u * ((up - down) * 0.5) + v * ((right - left) * 0.5) + turn
                lap = up + down + right + left - 4.0 * f
                state[slot, g, field, r] = (f - DT * tend + DT * VISC * lap) * ocean

    last = (STEPS - 1) % 2

    def forward_copies(g):
        found = []
        for k in range(1, n_mem):
            first = lax.rem(i_mem + k, n_mem) * per
            found.append(
                remote(
                    state.at[last, g, :, first // cols, :, pl.ds(pl.multiple_of(lax.rem(first, cols), 128), per)],
                    frecv.at[g, k],
                    f_ss.at[g, k],
                    f_rs.at[g, k],
                    to_mem(k),
                )
            )
        return found

    obs[pl.ds(0, 1), :] = values_ref[...]
    obs[pl.ds(1, 1), :] = errors_ref[...]
    obs_copies = [
        remote(obs, zobs.at[k], o_ss.at[k], o_rs.at[k], to_space(k)) for k in range(1, n_space)
    ]
    for g in range(groups):
        send_edges(0, g)
    for copy in obs_copies:
        copy.start()

    wanted = cells[...]
    for c in range(rows * cols // 128):
        index = lax.broadcasted_iota(jnp.int32, (128, n_obs), 0) + c * 128
        hot[pl.ds(c * 128, 128), :] = jnp.where(index == wanted, 1.0, 0.0).astype(jnp.bfloat16)
    split[...] = jnp.zeros_like(split)
    full[...] = jnp.zeros_like(full)
    xall[...] = jnp.zeros_like(xall)

    for step in range(STEPS):
        for g in range(groups):
            advance(step, g)
            if step < STEPS - 1:
                send_edges(step + 1, g)
            else:
                for r in range(rows):
                    h = state[last, g, 0, r]
                    for p in range(3):
                        part = h.astype(jnp.bfloat16).astype(jnp.float32)
                        split[pl.ds((p * groups + g) * SUB, gs), pl.ds(r * cols, cols)] = part
                        h = h - part
                if g < groups - 1:
                    for copy in forward_copies(g):
                        copy.start()

    three = jnp.dot(split[...].astype(jnp.bfloat16), hot[...], preferred_element_type=jnp.float32)
    size = groups * SUB
    mine = three[:size] + three[size : 2 * size] + three[2 * size :]
    for g in range(groups):
        picks[g] = mine[g * SUB : g * SUB + gs]
        zpicks[0, g] = mine[g * SUB : g * SUB + gs]
    z_copies = [
        remote(picks, zpicks.at[k], z_ss.at[k], z_rs.at[k], to_space(k)) for k in range(1, n_space)
    ]
    for copy in z_copies:
        copy.start()
    for copy in z_copies:
        copy.wait_recv()
    m_copies = [
        remote(zpicks, mpicks.at[k], m_ss.at[k], m_rs.at[k], to_mem(k)) for k in range(1, n_mem)
    ]
    for copy in m_copies:
        copy.start()
    for copy in forward_copies(groups - 1):
        copy.start()
    my_first = i_mem * per
    my_row = my_first // cols
    my_cols = pl.ds(pl.multiple_of(lax.rem(my_first, cols), 128), per)
    fwd = [forward_copies(g) for g in range(groups)]

    def collect(g):
        for f in range(3):
            full[f, pl.ds(g * SUB, gs), :] = state[last, g, f, my_row, :, my_cols]
        for k in range(1, n_mem):
            fwd[g][k - 1].wait_recv()
            for f in range(3):
                full[f, pl.ds((k * groups + g) * SUB, gs), :] = frecv[g, k, f]

    for g in range(groups - 1):
        collect(g)
    for copy in obs_copies:
        copy.wait_recv()
    for k in range(n_mem):
        if k > 0:
            m_copies[k - 1].wait_recv()
        for s in range(n_space):
            for g in range(groups):
                piece = zpicks[s, g] if k == 0 else mpicks[k, s, g]
                xall[pl.ds((k * groups + g) * SUB, gs), pl.ds(s * n_obs, n_obs)] = piece

    all_obs = [obs[...]] + [zobs[s] for s in range(1, n_space)]
    values = jnp.concatenate([pair[0:1] for pair in all_obs], axis=1)
    errors = jnp.concatenate([pair[1:2] for pair in all_obs], axis=1)
    valid = lax.rem(lax.broadcasted_iota(jnp.int32, (padded, n_space * n_obs), 0), SUB) < gs
    raw = xall[...]
    hmean = jnp.sum(raw, axis=0, keepdims=True) / members
    scaled = jnp.where(valid, (raw - hmean) / errors, 0.0)
    misfit = (values - hmean) / errors
    gram = dot(scaled, scaled, ((1,), (1,)))
    drive = jnp.sum(scaled * misfit, axis=1, keepdims=True)

    r_id = lax.broadcasted_iota(jnp.int32, (padded, padded), 0)
    c_id = lax.broadcasted_iota(jnp.int32, (padded, padded), 1)
    identity = jnp.where(r_id == c_id, 1.0, 0.0)
    system = identity + gram / (members - 1)
    squares = jnp.where(lax.rem(r_id, SUB) < gs, system * system, 0.0)
    norm_sq = jnp.sum(jnp.sum(squares, axis=1, keepdims=True), axis=0, keepdims=True)
    norm_scale = jnp.sqrt(norm_sq)
    iterate = system / norm_scale
    factor = 1.5 * identity - 0.5 * iterate
    carry = (dot(iterate, factor), factor)

    def sweep(_, carry):
        iterate, inverse = carry
        factor = 1.5 * identity - 0.5 * dot(inverse, iterate)
        return dot(iterate, factor), dot(factor, inverse)

    iterate, inverse = lax.fori_loop(0, NS_ITERS - 2, sweep, carry, unroll=padded <= 128)
    factor = 1.5 * identity - 0.5 * dot(inverse, iterate)
    weights = dot(factor, inverse) / jnp.sqrt(norm_scale)
    once = jnp.sum(weights * drive, axis=0, keepdims=True)
    mean_weight = jnp.sum(weights * once, axis=1, keepdims=True) / (members - 1)
    mixing = (weights + mean_weight).T

    collect(groups - 1)

    back = []
    for f in range(3):
        whole = full[f]
        center = jnp.sum(whole, axis=0, keepdims=True) / members
        done = center + dot(mixing, whole - center)
        for k in range(n_mem):
            for g in range(groups):
                piece = done[(k * groups + g) * SUB : (k * groups + g) * SUB + gs]
                if k == 0:
                    out[g, f, my_row, :, my_cols] = piece
                else:
                    rback[k, f, g] = piece
        for k in range(1, n_mem):
            copy = remote(
                rback.at[k, f],
                out.at[:, f, my_row, :, my_cols],
                b_ss.at[k, f],
                b_rs.at[k, f],
                to_mem(n_mem - k),
            )
            copy.start()
            back.append(copy)

    for step in range(STEPS):
        for g in range(groups):
            for copy in halo_copies(step, g):
                copy.wait_send()
    for copy in obs_copies + z_copies + m_copies + sum(fwd, []):
        copy.wait_send()
    for copy in back:
        copy.wait()


def local(ensemble, sea_depth, ocean_mask, observed_cells, observed_values, observed_error):
    n_mem = lax.axis_size("mem")
    n_space = lax.axis_size("space")
    local_members, fields, rows, cols = ensemble.shape
    n_obs = observed_cells.shape[1]
    gs = SUB if local_members % SUB == 0 else 1
    groups = local_members // gs
    per = rows * cols // n_mem
    padded = n_mem * groups * SUB
    dims = (n_mem, n_space, groups, gs, rows, cols, n_obs)
    ens = ensemble.reshape(groups, gs, fields, rows, cols).transpose(0, 2, 3, 1, 4)
    f32 = jnp.float32
    dma = pltpu.SemaphoreType.DMA
    result = pl.pallas_call(
        functools.partial(kernel, dims),
        out_shape=jax.ShapeDtypeStruct(ens.shape, f32),
        in_specs=[pl.BlockSpec(memory_space=pltpu.VMEM)] * 6,
        out_specs=pl.BlockSpec(memory_space=pltpu.VMEM),
        scratch_shapes=[
            pltpu.VMEM((2, groups, 3, rows, gs, cols), f32),
            pltpu.VMEM((rows + 2, gs, cols), f32),
            pltpu.VMEM((STEPS, groups, 2, 4, gs, cols), f32),
            pltpu.VMEM((STEPS, groups, 2, 4, gs, cols), f32),
            pltpu.VMEM((rows * cols, n_obs), jnp.bfloat16),
            pltpu.VMEM((3 * groups * SUB, rows * cols), f32),
            pltpu.VMEM((groups, gs, n_obs), f32),
            pltpu.VMEM((n_space, groups, gs, n_obs), f32),
            pltpu.VMEM((n_mem, n_space, groups, gs, n_obs), f32),
            pltpu.VMEM((2, n_obs), f32),
            pltpu.VMEM((n_space, 2, n_obs), f32),
            pltpu.VMEM((groups, n_mem, 3, gs, per), f32),
            pltpu.VMEM((3, padded, per), f32),
            pltpu.VMEM((padded, n_space * n_obs), f32),
            pltpu.VMEM((n_mem, 3, groups, gs, per), f32),
            dma((STEPS, groups, 2)),
            dma((STEPS, groups, 2)),
            dma((n_space,)),
            dma((n_space,)),
            dma((n_space,)),
            dma((n_space,)),
            dma((n_mem,)),
            dma((n_mem,)),
            dma((groups, n_mem)),
            dma((groups, n_mem)),
            dma((n_mem, 3)),
            dma((n_mem, 3)),
        ],
        compiler_params=pltpu.CompilerParams(
            collective_id=0, has_side_effects=True, vmem_limit_bytes=48 * 1024 * 1024
        ),
    )(ens, sea_depth, ocean_mask, observed_cells, observed_values, observed_error)
    return result.transpose(0, 3, 1, 2, 4).reshape(ensemble.shape)


def solution(mesh):
    return jax.shard_map(
        local,
        mesh=mesh,
        in_specs=(
            P("mem", None, "space", None),
            P("space", None),
            P("space", None),
            P("space", None),
            P("space", None),
            P("space", None),
        ),
        out_specs=P("mem", None, "space", None),
        check_vma=False,
    )
```
